256 devices in a mesh: pairs: 64 (over z, x, core), vecs: 4 (over y).
Axes of the slice: x: 4, y: 4, z: 8, core: 2. Of those that a mesh axis runs over, the one named last changes fastest.
Arguments:
- prev_vectors: float32 [32768, 2048], P('pairs', 'vecs'), may hold values from -1 to 1
- columns: float32 [32768, 512], P('pairs'), may hold values from -20 to 200, as said below
- pivots: int32 [2, 256], replicated, may hold values from 0 to 32767, as said below
Outputs:
- new_vectors: float32 [32768, 512], P('pairs')
The draws below stay inside these ranges and needn't reach their ends.
Inputs may be any that keep to these rules, and one draw needn't show every extreme that they name: All 2 x 256 pivots are distinct. The pivots of panel c lie in the c-th of 2 equal parts of the rows of each slab of 512 pairs. A slab holds at most 8 pivots of one panel, and in every panel some slab holds exactly 8. `columns`: in every panel the residual's pivot block is symmetric positive definite.
All inputs are finite; a program needn't handle non-finite values.
Results may differ from the reference program's by a relative error of at most 0.0001.
Values sent between devices are 32-bit elements; how exact they have to be, the bound alone decides.
No kernel may reach another device: no remote copies, remote signals or barrier semaphores. Data moves between devices by JAX's collectives and lax.ppermute only.
A program may use at most 64 MiB of HBM per device.

```python
import jax
import jax.numpy as jnp
from jax import lax

SLAB = 512
VECS = 2048
PANEL = 256
PANELS = 2
PAIRS = 32768
MOST = 8


def vector_table(key):
    subkey = jax.random.fold_in(key, 11)
    spread_scale = 0.5 ** 0.5 * VECS ** (-0.25)
    values = jnp.clip(jax.random.normal(subkey, (PAIRS, VECS), jnp.float32), -6.0, 6.0) * spread_scale
    return values


def pivot_table(key):
    slab_count = PAIRS // SLAB
    region = SLAB // PANELS
    stride = region // MOST
    tables = []
    for current in range(PANELS):
        subkey = jax.random.fold_in(key, 100 + current)
        keys = jax.random.split(subkey, 4)
        shuffle = jax.random.permutation(keys[0], slab_count * MOST).astype(jnp.int32)
        full_slab = jax.random.randint(keys[1], (), 0, slab_count)
        slot_ids = jnp.arange(slab_count * MOST, dtype=jnp.int32)
        scores = jnp.where(slot_ids // MOST == full_slab, slot_ids % MOST - MOST, shuffle)
        chosen = jnp.argsort(scores, stable=True)[:PANEL].astype(jnp.int32)
        chosen = chosen[jax.random.permutation(keys[2], PANEL)]
        owners = chosen // MOST
        within = chosen % MOST
        offsets = within * stride + jax.random.randint(keys[3], (PANEL,), 0, stride)
        tables.append(owners * SLAB + current * region + offsets)
    return jnp.stack(tables).astype(jnp.int32)


def draw_pivots(key, part):
    return pivot_table(key)


def draw_prev_vectors(key, part):
    return vector_table(key)


def draw_columns(key, part):
    pivot_all = pivot_table(key)
    vectors = vector_table(key)
    keys = jax.random.split(jax.random.fold_in(key, 23), 4)
    total_width = PANELS * PANEL
    base = jnp.clip(jax.random.normal(keys[0], (PAIRS, total_width), jnp.float32), -6.0, 6.0) * 3.0
    pivot_part = jnp.clip(jax.random.normal(keys[1], (PANELS * PANEL, total_width), jnp.float32), -6.0, 6.0) * 0.5
    base = base.at[pivot_all.reshape(-1)].set(pivot_part)
    for current in range(PANELS):
        pivot_ids = pivot_all[current]
        rows_known = vectors[pivot_ids]
        gram = jnp.dot(rows_known, rows_known.T, precision=lax.Precision.HIGHEST, preferred_element_type=jnp.float32)
        noise_key = jax.random.fold_in(keys[2], current)
        raw = jnp.clip(jax.random.normal(noise_key, (PANEL, PANEL), jnp.float32), -4.0, 4.0)
        noise = (raw + raw.T) * 0.5 ** 0.5
        diagonal = jax.random.uniform(jax.random.fold_in(keys[3], current), (PANEL,), jnp.float32, 72.0, 128.0)
        block = gram + noise + jnp.diag(diagonal) + 1.0
        column_ids = current * PANEL + jnp.arange(PANEL, dtype=jnp.int32)
        base = base.at[pivot_ids[:, None], column_ids[None, :]].set(block)
    return base


def setup_inputs(seed: int = 0) -> dict:
    key_list = jax.random.split(jax.random.key(seed), 4)
    return {
        "prev_vectors": draw_prev_vectors(jax.random.fold_in(key_list[3], 71), 0),
        "columns": draw_columns(jax.random.fold_in(key_list[3], 71), 0),
        "pivots": draw_pivots(jax.random.fold_in(key_list[3], 71), 0),
    }


def product(left, right):
    return jnp.dot(left.astype(jnp.float32), right.T.astype(jnp.float32), precision=lax.Precision.HIGHEST, preferred_element_type=jnp.float32)

def reference(prev_vectors, columns, pivots):
    blocks = []
    for current in range(PANELS):
        pivot_ids = pivots[current].astype(jnp.int32)
        products = product(prev_vectors, prev_vectors[pivot_ids])
        for block in blocks:
            products = products + product(block, block[pivot_ids])
        panel_columns = columns[:, current * PANEL:(current + 1) * PANEL]
        residual = panel_columns - products
        pivot_block = residual[pivot_ids]
        symmetric = 0.5 * (pivot_block + pivot_block.T)
        factor = jnp.linalg.cholesky(symmetric)
        solved = jax.scipy.linalg.solve_triangular(factor, residual.T, lower=True)
        blocks.append(solved.T)
    return jnp.concatenate(blocks, axis=1)
```

```python
import functools

import jax
import jax.numpy as jnp
from jax import lax
from jax.experimental import pallas as pl
from jax.experimental.pallas import tpu as pltpu
from jax.sharding import PartitionSpec as P


F32 = jnp.float32
BF16 = jnp.bfloat16
HIGHEST = lax.Precision.HIGHEST
SLAB, VLOC, PANEL, SLOTS = 512, 512, 256, 8
WIDE = VLOC + 128


def nt(a, b, precision=None):
    return lax.dot_general(
        a, b, (((1,), (1,)), ((), ())), precision=precision, preferred_element_type=F32
    )


def nn(a, b, precision=None):
    return lax.dot_general(
        a, b, (((1,), (0,)), ((), ())), precision=precision, preferred_element_type=F32
    )


def halves(a):
    hi = a.astype(BF16)
    return hi, (a - hi.astype(F32)).astype(BF16)


def nt3(a, b):
    return nt(a[0], b[0]) + (nt(a[0], b[1]) + nt(a[1], b[0]))


def select_kernel(meta, piv_ref, prev_ref, col_ref, out_ref):
    first = meta[0] * SLAB
    i = lax.broadcasted_iota(jnp.int32, (PANEL, PANEL), 0)
    j = lax.broadcasted_iota(jnp.int32, (PANEL, PANEL), 1)
    before = jnp.where(i < j, 1.0, 0.0)
    slot = lax.broadcasted_iota(jnp.int32, (SLOTS, PANEL), 0).astype(F32)
    lane = lax.broadcasted_iota(jnp.int32, (SLOTS, SLAB), 1).astype(F32)
    picks = []
    for c in range(2):
        local = piv_ref[c : c + 1, :] - first
        owned = (local >= 0) & (local < SLAB)
        ones = jnp.where(owned, 1.0, 0.0)
        rank = nn(jnp.broadcast_to(ones, (8, PANEL)), before)
        tag = jnp.where(owned, local.astype(F32) + 1.0, 0.0)
        hit = (rank == slot) & (jnp.broadcast_to(ones, (8, PANEL)) > 0.5)
        row = jnp.sum(jnp.where(hit, jnp.broadcast_to(tag, (8, PANEL)), 0.0), axis=1, keepdims=True)
        picks.append(jnp.where(lane == row - 1.0, 1.0, 0.0))
    pick = jnp.concatenate(picks, axis=0)
    out_ref[:, :VLOC] = nn(pick, prev_ref[...], HIGHEST)
    out_ref[:, VLOC:] = nn(pick, col_ref[...], HIGHEST)


def select(meta, pivots, prev, columns):
    return pl.pallas_call(
        select_kernel,
        out_shape=jax.ShapeDtypeStruct((2 * SLOTS, WIDE), F32),
        grid_spec=pltpu.PrefetchScalarGridSpec(
            num_scalar_prefetch=1,
            grid=(1,),
            in_specs=[
                pl.BlockSpec((2, PANEL), lambda g, m: (0, 0)),
                pl.BlockSpec((SLAB, VLOC), lambda g, m: (0, 0)),
                pl.BlockSpec((SLAB, 128), lambda g, m: (0, m[1])),
            ],
            out_specs=pl.BlockSpec((2 * SLOTS, WIDE), lambda g, m: (0, 0)),
        ),
        name="select",
    )(meta, pivots, prev, columns)


def order_kernel(meta, pos_ref, a_ref, b_ref, hi_ref, lo_ref, col_ref, t_ref):
    vec, core = meta[1], meta[2]
    n = a_ref.shape[0]
    lane = lax.broadcasted_iota(jnp.int32, (2 * PANEL, n), 1)
    pos = pos_ref[...]
    pick_a = jnp.where(lane == pos, 1.0, 0.0).astype(BF16)
    pick_b = jnp.where(lane == pos - n, 1.0, 0.0).astype(BF16)
    a_hi, a_lo = halves(a_ref[...])
    b_hi, b_lo = halves(b_ref[...])
    hi = nn(pick_a, a_hi) + nn(pick_b, b_hi)
    lo = nn(pick_a, a_lo) + nn(pick_b, b_lo)
    a_c, b_c = a_ref[:, VLOC:], b_ref[:, VLOC:]
    a_r = (a_c - a_hi[:, VLOC:].astype(F32)) - a_lo[:, VLOC:].astype(F32)
    b_r = (b_c - b_hi[:, VLOC:].astype(F32)) - b_lo[:, VLOC:].astype(F32)
    rest = nn(pick_a, a_r.astype(BF16)) + nn(pick_b, b_r.astype(BF16))
    col = hi[:, VLOC:] + (lo[:, VLOC:] + rest)
    col_ref[...] = col
    g_hi, g_lo = hi[:, :VLOC].astype(BF16), lo[:, :VLOC].astype(BF16)
    hi_ref[...] = g_hi
    lo_ref[...] = g_lo
    one = (g_hi[:PANEL], g_lo[:PANEL])
    gram = nt3(one, one)
    c1 = col[:PANEL]
    part = jnp.concatenate(
        [jnp.where(vec == 0, c1, 0.0), jnp.where(vec == 1, c1, 0.0)], axis=1
    ) - gram
    sym = 0.5 * (part + part.T)
    pack = jnp.concatenate([sym[:128, :128], sym[128:, :128], sym[128:, 128:]], axis=1)
    t_ref[...] = jnp.where(core == 0, pack[:64], pack[64:])


def order(meta, pos, a, b):
    return pl.pallas_call(
        order_kernel,
        out_shape=(
            jax.ShapeDtypeStruct((2 * PANEL, VLOC), BF16),
            jax.ShapeDtypeStruct((2 * PANEL, VLOC), BF16),
            jax.ShapeDtypeStruct((2 * PANEL, 128), F32),
            jax.ShapeDtypeStruct((64, 384), F32),
        ),
        in_specs=[pl.BlockSpec(memory_space=pltpu.SMEM)] + [pl.BlockSpec(memory_space=pltpu.VMEM)] * 3,
        name="order",
    )(meta, pos, a, b)


def products_kernel(meta, hi_ref, lo_ref, col_ref, prev_ref, t_ref, *p_refs):
    vec, core = meta[1], meta[2]
    g = (hi_ref[...], lo_ref[...])
    two = (g[0][PANEL:], g[1][PANEL:])
    gram = nt3(two, g)
    c2 = col_ref[PANEL:, :]
    part = jnp.concatenate([jnp.where(vec == q, c2, 0.0) for q in range(4)], axis=1) - gram
    sym = 0.5 * (part[:, PANEL:] + part[:, PANEL:].T)
    left = part[:, :PANEL]
    pack = jnp.concatenate(
        [left[:128], left[128:], sym[:128, :128], sym[128:, :128], sym[128:, 128:]], axis=1
    )
    t_ref[...] = jnp.where(core == 0, pack[:64], pack[64:])
    for k in range(4):
        rows = pl.ds(pl.multiple_of(lax.rem(vec + k, 4) * 128, 128), 128)
        p_refs[k][...] = nt3(halves(prev_ref[rows, :]), g)


def products(meta, hi, lo, col, prev):
    return pl.pallas_call(
        products_kernel,
        out_shape=(jax.ShapeDtypeStruct((64, 896), F32),)
        + (jax.ShapeDtypeStruct((128, 2 * PANEL), F32),) * 4,
        in_specs=[pl.BlockSpec(memory_space=pltpu.SMEM)] + [pl.BlockSpec(memory_space=pltpu.VMEM)] * 4,
        name="products",
    )(meta, hi, lo, col, prev)


def along_sublanes(x, k):
    return jnp.broadcast_to(x[k : k + 1, :], (8, 128))


def along_lanes(x, j):
    return jnp.broadcast_to(x[:, j : j + 1], (8, 128))


def inverse_factor_128(block):
    m = [block[8 * g : 8 * g + 8, :] for g in range(16)]
    lane = lax.broadcasted_iota(jnp.int32, (8, 128), 1)
    sub = lax.broadcasted_iota(jnp.int32, (8, 128), 0)
    out = []
    for k in range(16):
        cols = [along_lanes(m[k], 8 * k + i) for i in range(8)]
        below = [[along_lanes(m[g], 8 * k + i) for i in range(8)] for g in range(k + 1, 16)]
        inside = (lane >= 8 * k) & (lane < 8 * k + 8)
        p = jnp.where(inside, jnp.where(lane == sub + 8 * k, 1.0, 0.0), m[k])
        w = scale = None
        for j in range(8):
            d = along_sublanes(cols[j], j)
            r = 1.0 / d
            row = along_sublanes(p, j)
            wj = row * lax.rsqrt(d)
            w = wj if w is None else jnp.where(sub >= j, wj, w)
            scale = r if scale is None else jnp.where(sub >= j, r, scale)
            c = jnp.where(sub == j, 0.0, cols[j])
            for i in range(j + 1, 8):
                cols[i] = cols[i] - c * (along_sublanes(cols[i], j) * r)
            p = p - c * (row * r)
        z = p * scale
        out.append(jnp.where(lane <= sub + 8 * k, w, 0.0))
        zs = [along_sublanes(z, i) for i in range(8)]
        for n, g in enumerate(range(k + 1, 16)):
            f = below[n]
            s0 = (f[0] * zs[0] + f[1] * zs[1]) + (f[2] * zs[2] + f[3] * zs[3])
            s1 = (f[4] * zs[4] + f[5] * zs[5]) + (f[6] * zs[6] + f[7] * zs[7])
            m[g] = jnp.where(inside, 0.0, m[g]) - (s0 + s1)
    return jnp.concatenate(out, axis=0)


def inverse_factor_256(a_ref, w_ref):
    def step(i, carry):
        @pl.when(i == 1)
        def _():
            w00 = w_ref[:128, :128]
            l10 = nt(a_ref[:, 128:256], w00, HIGHEST)
            a_ref[:, 128:256] = l10
            a_ref[:, 256:] = a_ref[:, 256:] - nt(l10, l10, HIGHEST)

        at = pl.multiple_of(i * 256, 128)
        to = pl.multiple_of(i * 128, 128)
        w_ref[pl.ds(to, 128), pl.ds(to, 128)] = inverse_factor_128(a_ref[:, pl.ds(at, 128)])
        return carry

    lax.fori_loop(0, 2, step, 0)
    w_ref[:128, 128:] = jnp.zeros((128, 128), F32)
    mid = nn(a_ref[:, 128:256], w_ref[:128, :128], HIGHEST)
    w_ref[128:, :128] = -nn(w_ref[128:, 128:], mid, HIGHEST)


def both_halves(core, mine, other):
    return jnp.where(core == 0, mine, other), jnp.where(core == 0, other, mine)


def first_kernel(meta, mine_ref, other_ref, w_ref, a_ref):
    top, low = both_halves(meta[2], mine_ref[...], other_ref[...])
    a_ref[:64, :] = top
    a_ref[64:, :] = low
    inverse_factor_256(a_ref, w_ref)


def first_panel(meta, mine, other):
    return pl.pallas_call(
        first_kernel,
        out_shape=jax.ShapeDtypeStruct((PANEL, PANEL), F32),
        in_specs=[pl.BlockSpec(memory_space=pltpu.SMEM)] + [pl.BlockSpec(memory_space=pltpu.VMEM)] * 2,
        scratch_shapes=[pltpu.VMEM((128, 384), F32)],
        cost_estimate=pl.CostEstimate(flops=4_000_000_000, bytes_accessed=20_000_000, transcendentals=0),
        name="first_panel",
    )(meta, mine, other)


def second_kernel(meta, mine_ref, other_ref, w1_ref, w_ref, l_ref, a_ref):
    top, low = both_halves(meta[2], mine_ref[...], other_ref[...])
    w1 = w1_ref[...]
    l_ref[:64, :] = nt(top[:, :256], w1, HIGHEST)
    l_ref[64:128, :] = nt(low[:, :256], w1, HIGHEST)
    l_ref[128:192, :] = nt(top[:, 256:512], w1, HIGHEST)
    l_ref[192:, :] = nt(low[:, 256:512], w1, HIGHEST)
    l_top, l_low = l_ref[:128, :], l_ref[128:, :]
    a_ref[:64, :] = top[:, 512:]
    a_ref[64:, :] = low[:, 512:]
    a_ref[:, :128] = a_ref[:, :128] - nt(l_top, l_top, HIGHEST)
    a_ref[:, 128:256] = a_ref[:, 128:256] - nt(l_low, l_top, HIGHEST)
    a_ref[:, 256:] = a_ref[:, 256:] - nt(l_low, l_low, HIGHEST)
    inverse_factor_256(a_ref, w_ref)


def second_panel(meta, mine, other, w1):
    return pl.pallas_call(
        second_kernel,
        out_shape=(jax.ShapeDtypeStruct((PANEL, PANEL), F32),) * 2,
        in_specs=[pl.BlockSpec(memory_space=pltpu.SMEM)] + [pl.BlockSpec(memory_space=pltpu.VMEM)] * 3,
        scratch_shapes=[pltpu.VMEM((128, 384), F32)],
        cost_estimate=pl.CostEstimate(flops=4_000_000_000, bytes_accessed=20_000_000, transcendentals=0),
        name="second_panel",
    )(meta, mine, other, w1)


def solve_kernel(meta, r0, r1, r2, r3, w1_ref, l_ref, w2_ref, out_ref):
    vec = meta[1]
    w1, l21, w2 = halves(w1_ref[...]), halves(l_ref[...]), halves(w2_ref[...])
    for k, r in enumerate((r0, r1, r2, r3)):
        rows = pl.ds(pl.multiple_of(lax.rem(vec + 4 - k, 4) * 128, 128), 128)
        v1 = nt3(halves(r[:, :PANEL]), w1)
        out_ref[rows, :PANEL] = v1
        rest = r[:, PANEL:] - nt3(halves(v1), l21)
        out_ref[rows, PANEL:] = nt3(halves(rest), w2)


def solve(meta, chunks, w1, l21, w2):
    return pl.pallas_call(
        solve_kernel,
        out_shape=jax.ShapeDtypeStruct((SLAB, 2 * PANEL), F32),
        in_specs=[pl.BlockSpec(memory_space=pltpu.SMEM)] + [pl.BlockSpec(memory_space=pltpu.VMEM)] * 7,
        name="solve",
    )(meta, *chunks, w1, l21, w2)


def over_pairs(value, move):
    perm = []
    for i in range(64):
        z, x, c = i // 8, (i // 2) % 4, i % 2
        z, x, c = move(z, x, c)
        perm.append((i, (z % 8) * 8 + (x % 4) * 2 + c))
    return lax.ppermute(value, "pairs", perm)


def over_vecs(value, k):
    return lax.ppermute(value, "vecs", [(i, (i + k) % 4) for i in range(4)])


def sibling(value):
    return over_pairs(value, lambda z, x, c: (z, x, 1 - c))


def gather(selected):
    chip = jnp.concatenate([selected, sibling(selected)], axis=0)
    parts = [selected]
    for k in (1, 2, 3):
        parts.append(over_pairs(chip, lambda z, x, c, k=k: (z + k * (1 - 2 * c), x, c)))
    parts.append(over_pairs(selected, lambda z, x, c: (z + 4, x, c)))
    line = jnp.concatenate(parts, axis=0)
    plane = jnp.concatenate(
        [line] + [over_pairs(line, lambda z, x, c, k=k: (z, x + k, c)) for k in (1, 2, 3)], axis=0
    )
    return plane, sibling(plane)


def positions(pivots, me):
    z, x, c = me // 8, (me // 2) % 4, me % 2
    owner = pivots // SLAB
    zo, xo, co = owner // 8, (owner // 2) % 4, owner % 2
    order_ids = jnp.arange(PANEL, dtype=jnp.int32)
    earlier = (owner[:, :, None] == owner[:, None, :]) & (
        order_ids[None, None, :] < order_ids[None, :, None]
    )
    rank = jnp.sum(earlier.astype(jnp.int32), axis=2)
    back = (z - zo + 8) % 8
    holder = jnp.where((back == 0) | (back == 4), co, jnp.where(back < 4, 0, 1))
    steps = jnp.where(back < 4, back, 8 - back)
    inner = 16 + (steps - 1) * 32 + 16 * (co != holder).astype(jnp.int32)
    off = jnp.where(back == 0, 0, jnp.where(back == 4, 112, inner))
    block = (holder != c).astype(jnp.int32)
    panel = jnp.arange(2, dtype=jnp.int32)[:, None]
    pos = block * 512 + ((x - xo + 4) % 4) * 128 + off + panel * SLOTS + rank
    return pos.reshape(2 * PANEL, 1)


def reduced(own):
    r1, r2, r3 = [over_vecs(own, k) for k in (1, 2, 3)]
    return (own + r2) + (r1 + r3)


def body(prev_vectors, columns, pivots):
    me = lax.axis_index("pairs")
    vec = lax.axis_index("vecs")
    meta = jnp.stack([me, vec, me % 2]).astype(jnp.int32)
    selected = select(meta, pivots, prev_vectors, columns)
    pos = positions(pivots, me)
    plane, other = gather(selected)
    hi, lo, col, t1 = order(meta, pos, plane, other)
    t1 = reduced(t1)
    t1_other = sibling(t1)
    t2, p0, p1, p2, p3 = products(meta, hi, lo, col, prev_vectors)
    w1 = first_panel(meta, t1, t1_other)
    t2 = reduced(t2)
    t2_other = sibling(t2)
    q1, q2, q3 = over_vecs(p1, 1), over_vecs(p2, 2), over_vecs(p3, 3)
    mine = lax.dynamic_slice_in_dim(columns, vec * 128, 128, 0)
    rest = mine - ((p0 + q2) + (q1 + q3))
    chunks = [rest] + [over_vecs(rest, k) for k in (1, 2, 3)]
    w2, l21 = second_panel(meta, t2, t2_other, w1)
    return solve(meta, chunks, w1, l21, w2)


def solution(mesh):
    placed = (P("pairs", "vecs"), P("pairs", None), P())
    return jax.shard_map(
        body, mesh=mesh, in_specs=placed, out_specs=P("pairs", None), check_vma=False
    )
```

```python
import jax
import jax.numpy as jnp
from jax import lax
from jax.experimental import pallas as pl
from jax.experimental.pallas import tpu as pltpu
from jax.sharding import PartitionSpec as P


F32 = jnp.float32
BF16 = jnp.bfloat16
HIGHEST = lax.Precision.HIGHEST
SLAB, VLOC, PANEL, SLOTS = 512, 512, 256, 8
WIDE = VLOC + 128
GRANT = 24 * 1024 * 1024


def nt(a, b, precision=None):
    return lax.dot_general(
        a, b, (((1,), (1,)), ((), ())), precision=precision, preferred_element_type=F32
    )


def nn(a, b, precision=None):
    return lax.dot_general(
        a, b, (((1,), (0,)), ((), ())), precision=precision, preferred_element_type=F32
    )


def halves(a):
    hi = a.astype(BF16)
    return hi, (a - hi.astype(F32)).astype(BF16)


def nt3(a, b):
    return nt(a[0], b[0]) + (nt(a[0], b[1]) + nt(a[1], b[0]))


def thirds(a):
    hi, mid = halves(a)
    return hi, mid, ((a - hi.astype(F32)) - mid.astype(F32)).astype(BF16)


def picked(pick, parts):
    hi, mid, lo = [nn(pick, part) for part in parts]
    return hi + (mid + lo)


def select_kernel(piv_ref, prev_ref, col_hbm, out_ref, col_ref, sem):
    at = pl.multiple_of(lax.axis_index("vecs") * 128, 128)
    copy = pltpu.make_async_copy(col_hbm.at[:, pl.ds(at, 128)], col_ref, sem)
    copy.start()
    first = lax.axis_index("pairs") * SLAB
    i = lax.broadcasted_iota(jnp.int32, (PANEL, PANEL), 0)
    j = lax.broadcasted_iota(jnp.int32, (PANEL, PANEL), 1)
    before = jnp.where(i < j, 1.0, 0.0).astype(BF16)
    slot = lax.broadcasted_iota(jnp.int32, (SLOTS, PANEL), 0).astype(F32)
    lane = lax.broadcasted_iota(jnp.int32, (SLOTS, SLAB), 1).astype(F32)
    picks = []
    for c in range(2):
        local = piv_ref[c : c + 1, :] - first
        owned = (local >= 0) & (local < SLAB)
        ones = jnp.broadcast_to(jnp.where(owned, 1.0, 0.0), (SLOTS, PANEL))
        tag = jnp.broadcast_to(jnp.where(owned, local.astype(F32) + 1.0, 0.0), (SLOTS, PANEL))
        rank = nn(ones.astype(BF16), before)
        hit = (rank == slot) & (ones > 0.5)
        row = jnp.sum(jnp.where(hit, tag, 0.0), axis=1, keepdims=True)
        picks.append(jnp.where(lane == row - 1.0, 1.0, 0.0))
    pick = jnp.concatenate(picks, axis=0).astype(BF16)
    out_ref[:, :VLOC] = picked(pick, thirds(prev_ref[...]))
    copy.wait()
    out_ref[:, VLOC:] = picked(pick, thirds(col_ref[...]))


VMEM = pl.BlockSpec(memory_space=pltpu.VMEM)
SMEM = pl.BlockSpec(memory_space=pltpu.SMEM)


def select(pivots, prev, columns):
    return pl.pallas_call(
        select_kernel,
        out_shape=jax.ShapeDtypeStruct((2 * SLOTS, WIDE), F32),
        in_specs=[VMEM, VMEM, pl.BlockSpec(memory_space=pl.ANY)],
        scratch_shapes=[pltpu.VMEM((SLAB, 128), F32), pltpu.SemaphoreType.DMA],
        compiler_params=pltpu.CompilerParams(vmem_limit_bytes=GRANT),
        name="select",
    )(pivots, prev, columns)


def in_pivot_order(pos, a_ref, b_ref):
    both = jnp.concatenate([a_ref[...], b_ref[...]], axis=0)
    lane = lax.broadcasted_iota(jnp.int32, (PANEL, both.shape[0]), 1)
    pick = jnp.where(lane == pos, 1.0, 0.0).astype(BF16)
    hi, lo = [nn(pick, part).astype(BF16) for part in halves(both[:, :VLOC])]
    return hi, lo, picked(pick, thirds(both[:, VLOC:]))


def my_rows(core, pack):
    return jnp.where(core == 0, pack[:64], pack[64:])


def order_kernel(meta, pos_ref, a_ref, b_ref, hi_ref, lo_ref, t_ref):
    vec, core = meta[1], meta[2]
    hi, lo, col = in_pivot_order(pos_ref[...], a_ref, b_ref)
    hi_ref[...] = hi
    lo_ref[...] = lo
    gram = nt3((hi, lo), (hi, lo))
    part = jnp.concatenate([jnp.where(vec == q, col, 0.0) for q in range(2)], axis=1) - gram
    sym = 0.5 * (part + part.T)
    t_ref[...] = my_rows(
        core, jnp.concatenate([sym[:128, :128], sym[128:, :128], sym[128:, 128:]], axis=1)
    )


def order(meta, pos, a, b):
    return pl.pallas_call(
        order_kernel,
        out_shape=(jax.ShapeDtypeStruct((PANEL, VLOC), BF16),) * 2
        + (jax.ShapeDtypeStruct((64, 384), F32),),
        in_specs=[SMEM] + [VMEM] * 3,
        cost_estimate=pl.CostEstimate(flops=500_000_000, bytes_accessed=3_000_000, transcendentals=0),
        compiler_params=pltpu.CompilerParams(vmem_limit_bytes=GRANT),
        name="order",
    )(meta, pos, a, b)


def chunk_rows(vec, k):
    return pl.ds(pl.multiple_of((vec ^ k) * 128, 128), 128)


def slab_products(vec, prev_ref, g, p_refs):
    mine = jnp.concatenate([prev_ref[chunk_rows(vec, k), :] for k in range(4)], axis=0)
    out = nt3(halves(mine), g)
    for k in range(4):
        p_refs[k][...] = out[128 * k : 128 * k + 128]


def products_kernel(meta, hi_ref, lo_ref, prev_ref, *p_refs):
    slab_products(meta[1], prev_ref, (hi_ref[...], lo_ref[...]), p_refs)


def products(meta, hi, lo, prev):
    return pl.pallas_call(
        products_kernel,
        out_shape=(jax.ShapeDtypeStruct((128, PANEL), F32),) * 4,
        in_specs=[SMEM] + [VMEM] * 3,
        cost_estimate=pl.CostEstimate(flops=500_000_000, bytes_accessed=3_000_000, transcendentals=0),
        compiler_params=pltpu.CompilerParams(vmem_limit_bytes=GRANT),
        name="products",
    )(meta, hi, lo, prev)


def later_kernel(meta, pos_ref, a_ref, b_ref, hi_ref, lo_ref, prev_ref, t_ref, *p_refs):
    vec, core = meta[1], meta[2]
    hi, lo, col = in_pivot_order(pos_ref[...], a_ref, b_ref)
    g = (
        jnp.concatenate([hi_ref[...], hi], axis=0),
        jnp.concatenate([lo_ref[...], lo], axis=0),
    )
    part = jnp.concatenate([jnp.where(vec == q, col, 0.0) for q in range(4)], axis=1) - nt3((hi, lo), g)
    left, right = part[:, :PANEL], part[:, PANEL:]
    sym = 0.5 * (right + right.T)
    t_ref[...] = my_rows(
        core,
        jnp.concatenate(
            [left[:128], left[128:], sym[:128, :128], sym[128:, :128], sym[128:, 128:]], axis=1
        ),
    )
    slab_products(vec, prev_ref, (hi, lo), p_refs)


def later(meta, pos, a, b, hi, lo, prev):
    return pl.pallas_call(
        later_kernel,
        out_shape=(jax.ShapeDtypeStruct((64, 896), F32),)
        + (jax.ShapeDtypeStruct((128, PANEL), F32),) * 4,
        in_specs=[SMEM] + [VMEM] * 6,
        cost_estimate=pl.CostEstimate(flops=900_000_000, bytes_accessed=4_000_000, transcendentals=0),
        compiler_params=pltpu.CompilerParams(vmem_limit_bytes=GRANT),
        name="later",
    )(meta, pos, a, b, hi, lo, prev)


def along_sublanes(x, k):
    return jnp.broadcast_to(x[k : k + 1, :], (8, 128))


def along_lanes(x, j):
    return jnp.take_along_axis(x, jnp.full((8, 128), j, jnp.int32), axis=1)


def inverse_of(d):
    r = pltpu.reciprocal(d, approx=True)
    return r * (2.0 - d * r)


def weighted(f, z):
    s0 = (f[0] * z[0] + f[1] * z[1]) + (f[2] * z[2] + f[3] * z[3])
    s1 = (f[4] * z[4] + f[5] * z[5]) + (f[6] * z[6] + f[7] * z[7])
    return s0 + s1


def inverse_factor(m_ref, w_ref):
    lane = lax.broadcasted_iota(jnp.int32, (8, 128), 1)
    sub = lax.broadcasted_iota(jnp.int32, (8, 128), 0)
    tiles = (slice(0, 128), slice(128, 256))
    for s in range(8):
        t, o, r0 = s // 4, 32 * (s % 4), 32 * s
        p = [[m_ref[r0 + 8 * g : r0 + 8 * g + 8, tile] for tile in tiles] for g in range(4)]
        for k in range(4):
            c0 = o + 8 * k
            cols = [along_lanes(p[k][t], c0 + i) for i in range(8)]
            outer = {g: [along_lanes(p[g][t], c0 + i) for i in range(8)] for g in range(4) if g != k}
            inside = (lane >= c0) & (lane < c0 + 8)
            q = list(p[k])
            q[t] = jnp.where(inside, jnp.where(lane == sub + c0, 1.0, 0.0), q[t])
            w, scale = [None, None], None
            for j in range(8):
                d = along_sublanes(cols[j], j)
                r = inverse_of(d)
                root = lax.rsqrt(d)
                scale = r if scale is None else jnp.where(sub >= j, r, scale)
                c = jnp.where(sub == j, 0.0, cols[j]) * r
                for i in range(j + 1, 8):
                    cols[i] = cols[i] - c * along_sublanes(cols[i], j)
                for u in range(2):
                    row = along_sublanes(q[u], j)
                    if u <= t:
                        w[u] = row * root if w[u] is None else jnp.where(sub >= j, row * root, w[u])
                    q[u] = q[u] - c * row
            p[k] = [q[u] * scale for u in range(2)]
            rows = slice(r0 + 8 * k, r0 + 8 * k + 8)
            for u in range(2):
                if u < t:
                    w_ref[rows, tiles[u]] = w[u]
                elif u == t:
                    w_ref[rows, tiles[u]] = jnp.where(lane <= sub + c0, w[u], 0.0)
                else:
                    w_ref[rows, tiles[u]] = jnp.zeros((8, 128), F32)
            zs = [[along_sublanes(p[k][u], i) for i in range(8)] for u in range(2)]
            for g in outer:
                for u in range(2):
                    base = jnp.where(inside, 0.0, p[g][u]) if u == t else p[g][u]
                    p[g][u] = base - weighted(outer[g], zs[u])
        if s == 7:
            break
        z = [jnp.concatenate(p[g], axis=1) for g in range(4)]
        if o:
            z.insert(0, jnp.zeros((o, PANEL), F32))
        if o < 96:
            z.append(jnp.zeros((96 - o, PANEL), F32))
        z = jnp.concatenate(z, axis=0)
        for lo, hi in ((r0 + 32, r0 + 64), (r0 + 64, PANEL)):
            if lo == hi:
                continue
            at = lax.broadcasted_iota(jnp.int32, (hi - lo, 128), 1)
            block = (at >= o) & (at < o + 32)
            update = nn(jnp.where(block, m_ref[lo:hi, tiles[t]], 0.0), z, HIGHEST)
            for u in range(2):
                old = m_ref[lo:hi, tiles[u]]
                if u == t:
                    old = jnp.where(block, 0.0, old)
                m_ref[lo:hi, tiles[u]] = old - update[:, tiles[u]]


def both_halves(core, mine, other):
    return jnp.where(core == 0, mine, other), jnp.where(core == 0, other, mine)


COSTLY = pl.CostEstimate(flops=4_000_000_000, bytes_accessed=20_000_000, transcendentals=0)


def first_kernel(meta, mine_ref, other_ref, w_ref, m_ref):
    a = jnp.concatenate(both_halves(meta[2], mine_ref[...], other_ref[...]), axis=0)
    m_ref[:128, :128] = a[:, :128]
    m_ref[128:, :128] = a[:, 128:256]
    m_ref[:128, 128:] = a[:, 128:256].T
    m_ref[128:, 128:] = a[:, 256:]
    inverse_factor(m_ref, w_ref)


def first_panel(meta, mine, other):
    return pl.pallas_call(
        first_kernel,
        out_shape=jax.ShapeDtypeStruct((PANEL, PANEL), F32),
        in_specs=[SMEM] + [VMEM] * 2,
        scratch_shapes=[pltpu.VMEM((PANEL, PANEL), F32)],
        cost_estimate=COSTLY,
        compiler_params=pltpu.CompilerParams(vmem_limit_bytes=GRANT),
        name="first_panel",
    )(meta, mine, other)


def second_kernel(meta, mine_ref, other_ref, w1_ref, w_ref, l_ref, m_ref):
    a = jnp.concatenate(both_halves(meta[2], mine_ref[...], other_ref[...]), axis=0)
    left = jnp.concatenate([a[:, :256], a[:, 256:512]], axis=0)
    l21 = nt(left, w1_ref[...], HIGHEST)
    l_ref[...] = l21
    m_ref[:128, :128] = a[:, 512:640]
    m_ref[128:, :128] = a[:, 640:768]
    m_ref[:128, 128:] = a[:, 640:768].T
    m_ref[128:, 128:] = a[:, 768:]
    m_ref[...] = m_ref[...] - nt(l21, l21, HIGHEST)
    inverse_factor(m_ref, w_ref)


def second_panel(meta, mine, other, w1):
    return pl.pallas_call(
        second_kernel,
        out_shape=(jax.ShapeDtypeStruct((PANEL, PANEL), F32),) * 2,
        in_specs=[SMEM] + [VMEM] * 3,
        scratch_shapes=[pltpu.VMEM((PANEL, PANEL), F32)],
        cost_estimate=COSTLY,
        compiler_params=pltpu.CompilerParams(vmem_limit_bytes=GRANT),
        name="second_panel",
    )(meta, mine, other, w1)


def solve_kernel(meta, r0, r1, r2, r3, w1_ref, l_ref, w2_ref, out_ref):
    vec = meta[1]
    chunks = (r0, r1, r2, r3)
    one = jnp.concatenate([r[:, :PANEL] for r in chunks], axis=0)
    two = jnp.concatenate([r[:, PANEL:] for r in chunks], axis=0)
    v1 = nt3(halves(one), halves(w1_ref[...]))
    v2 = nt3(halves(two - nt3(halves(v1), halves(l_ref[...]))), halves(w2_ref[...]))
    for k in range(4):
        rows = chunk_rows(vec, k)
        out_ref[rows, :PANEL] = v1[128 * k : 128 * k + 128]
        out_ref[rows, PANEL:] = v2[128 * k : 128 * k + 128]


def solve(meta, chunks, w1, l21, w2):
    return pl.pallas_call(
        solve_kernel,
        out_shape=jax.ShapeDtypeStruct((SLAB, 2 * PANEL), F32),
        in_specs=[SMEM] + [VMEM] * 7,
        compiler_params=pltpu.CompilerParams(vmem_limit_bytes=GRANT),
        name="solve",
    )(meta, *chunks, w1, l21, w2)


def over_pairs(value, move):
    perm = []
    for i in range(64):
        z, x, c = move(i // 8, (i // 2) % 4, i % 2)
        perm.append((i, (z % 8) * 8 + (x % 4) * 2 + c))
    return lax.ppermute(value, "pairs", perm)


def over_vecs(value, k):
    return lax.ppermute(value, "vecs", [(i, i ^ k) for i in range(4)])


def sibling(value):
    return over_pairs(value, lambda z, x, c: (z, x, 1 - c))


def gather(selected):
    one, two = selected[:SLOTS], selected[SLOTS:]
    there = sibling(selected)
    chip = jnp.concatenate([one, there[:SLOTS], two, there[SLOTS:]], axis=0)
    z = [over_pairs(chip, lambda z, x, c, k=k: (z ^ (k + 4 * c), x, c)) for k in (1, 2, 3)]
    far = over_pairs(selected, lambda z, x, c: (z ^ 4, x, c))
    lines = (
        jnp.concatenate([one] + [v[: 2 * SLOTS] for v in z] + [far[:SLOTS]], axis=0),
        jnp.concatenate([two] + [v[2 * SLOTS :] for v in z] + [far[SLOTS:]], axis=0),
    )
    planes = []
    for line in lines:
        plane = jnp.concatenate(
            [line]
            + [over_pairs(line, lambda z, x, c, k=k: (z, x ^ k, c)) for k in (1, 2, 3)],
            axis=0,
        )
        planes.append((plane, sibling(plane)))
    return planes


def positions(pivots, me):
    z, x, c = me // 8, (me // 2) % 4, me % 2
    owner = pivots // SLAB
    zo, xo, co = owner // 8, (owner // 2) % 4, owner % 2
    order_ids = jnp.arange(PANEL, dtype=jnp.int32)
    earlier = (owner[:, :, None] == owner[:, None, :]) & (
        order_ids[None, None, :] < order_ids[None, :, None]
    )
    rank = jnp.sum(earlier.astype(jnp.int32), axis=2)
    away = z ^ zo
    holder = jnp.where(away % 4 == 0, co, away // 4)
    inner = 1 + (away % 4 - 1) * 2 + (co != holder).astype(jnp.int32)
    place = jnp.where(away == 0, 0, jnp.where(away == 4, 7, inner))
    block = (holder != c).astype(jnp.int32)
    return ((block * 4 + (x ^ xo)) * 8 + place) * SLOTS + rank


def summed(r):
    return (r[0] + r[2]) + (r[1] + r[3])


def reduced(own):
    return summed([own] + [over_vecs(own, k) for k in (1, 2, 3)])


def body(prev_vectors, columns, pivots):
    me = lax.axis_index("pairs")
    vec = lax.axis_index("vecs")
    selected = select(pivots, prev_vectors, columns)
    meta = jnp.stack([me, vec, me % 2]).astype(jnp.int32)
    pos = positions(pivots, me)
    (a1, b1), (a2, b2) = gather(selected)
    hi, lo, t1 = order(meta, pos[0][:, None], a1, b1)
    t1 = reduced(t1)
    p1 = products(meta, hi, lo, prev_vectors)
    q1 = [p1[0]] + [over_vecs(p1[k], k) for k in (1, 2, 3)]
    t2, *p2 = later(meta, pos[1][:, None], a2, b2, hi, lo, prev_vectors)
    t1_other = sibling(t1)
    t2 = reduced(t2)
    q2 = [p2[0]] + [over_vecs(p2[k], k) for k in (1, 2, 3)]
    w1 = first_panel(meta, t1, t1_other)
    t2_other = sibling(t2)
    mine = lax.dynamic_slice_in_dim(columns, vec * 128, 128, 0)
    rest = mine - jnp.concatenate([summed(q1), summed(q2)], axis=1)
    chunks = [rest] + [over_vecs(rest, k) for k in (1, 2, 3)]
    w2, l21 = second_panel(meta, t2, t2_other, w1)
    return solve(meta, chunks, w1, l21, w2)


def solution(mesh):
    placed = (P("pairs", "vecs"), P("pairs", None), P())
    return jax.shard_map(
        body, mesh=mesh, in_specs=placed, out_specs=P("pairs", None), check_vma=False
    )
```
